512 devices in a mesh: replica: 32 (over z_lo, y, core), tensor: 16 (over z_hi, x).
Axes of the slice: x: 4, y: 4, z: 16 (z_hi: 4, z_lo: 4; z = z_hi * 4 + z_lo), core: 2. Of those that a mesh axis runs over, the one named last changes fastest.
Arguments:
- queries: bfloat16 [1024, 4, 8192], P('replica', None, 'tensor'), may hold values from -64 to 64
- new_keys: bfloat16 [1024, 4, 2048], P('replica', None, 'tensor'), may hold values from -6 to 6, as said below
- new_values: bfloat16 [1024, 4, 2048], P('replica', None, 'tensor'), may hold values from -6 to 6, as said below
- cache_keys: bfloat16 [1024, 128, 2048], P('replica', None, 'tensor'), may hold values from -6 to 6, as said below
- cache_values: bfloat16 [1024, 128, 2048], P('replica', None, 'tensor'), may hold values from -6 to 6, as said below
- serve_lists: int32 [32, 32], replicated, may hold values from 0 to 1023, as said below
- turn_lens: int32 [1024], replicated, may hold values from 1 to 4, 2560 in all
- cache_lens: int32 [1024], P('replica'), may hold values from 1 to 128, 65536 in all
- owner_map: int32 [32], replicated, may hold values from 0 to 31, each once
- new_wo: bfloat16 [32, 256, 5120], P('replica', 'tensor'), may hold values from -0.0625 to 0.0625
Outputs:
- projected: bfloat16 [32, 128, 5120], P('replica', 'tensor')
The draws below stay inside these ranges and needn't reach their ends.
Inputs may be any that keep to these rules, and one draw needn't show every extreme that they name: `serve_lists`: row r lists the trajectories whose caches replica r holds, one a slot; every trajectory id appears once, and each row holds exactly one id of every block of 32 consecutive ids. `new_keys`: column block j equals column block (j // 2) * 2: 8 distinct heads, each stored 2 times. `new_values`: column block j equals column block (j // 2) * 2: 8 distinct heads, each stored 2 times. `cache_keys`: column block j equals column block (j // 2) * 2: 8 distinct heads, each stored 2 times. `cache_values`: column block j equals column block (j // 2) * 2: 8 distinct heads, each stored 2 times.
All inputs are finite; a program needn't handle non-finite values. No bound on the sum of `cache_lens` on one device may be relied on, other than what follows from the above.
Results may differ from the reference program's by a relative error of at most 0.019.
Values may be sent and summed in bfloat16 or wider, within the bound.
No kernel may reach another device: no remote copies, remote signals or barrier semaphores. Data moves between devices by JAX's collectives and lax.ppermute only.
A program may use at most 64 MiB of HBM per device.

```python
import math
import jax
import jax.numpy as jnp
import numpy as np
from jax import lax

D = 5120
Q_HEADS = 64
KV_HEADS = 8
HD = 128
TURN = 4
CL = 128
NTRAJ = 1024
QH_DEV = 4
KV_COLS = 2048
KV_REP = 2
OWN_ROWS = 16
N_REPLICA = 32
N_TENSOR = 16


def routing(key):
    base = jax.random.fold_in(key, 11)
    shift_perm = jax.random.permutation(jax.random.fold_in(base, 1), N_REPLICA).astype(jnp.int32)
    pick_perm = jax.random.permutation(jax.random.fold_in(base, 2), N_REPLICA).astype(jnp.int32)
    offset_perm = jax.random.permutation(jax.random.fold_in(base, 3), N_REPLICA).astype(jnp.int32)
    replica_ids = jnp.arange(N_REPLICA, dtype=jnp.int32)[:, None]
    slot_ids = jnp.arange(N_REPLICA, dtype=jnp.int32)[None, :]
    source = (shift_perm[slot_ids] + replica_ids) % N_REPLICA
    chosen = pick_perm[(replica_ids + offset_perm[source]) % N_REPLICA]
    return (source * N_REPLICA + chosen).astype(jnp.int32)


def draw_serve_lists(key, part):
    return routing(key)


def copy_heads(distinct):
    lead = distinct.shape[:-1]
    shaped = distinct.reshape(lead + (KV_HEADS, 1, HD))
    copied = jnp.broadcast_to(shaped, lead + (KV_HEADS, KV_REP, HD))
    return copied.reshape(lead + (KV_COLS,))


def head_draw(key, rows):
    shape = (NTRAJ, rows, KV_HEADS * HD)
    drawn = jnp.clip(jax.random.normal(key, shape, jnp.float32), -6.0, 6.0)
    return copy_heads(drawn)


def base_keys(key):
    return head_draw(jax.random.fold_in(key, 21), TURN)


def draw_new_keys(key, part):
    return base_keys(key).astype(jnp.bfloat16)


def draw_new_values(key, part):
    return head_draw(jax.random.fold_in(key, 61), TURN).astype(jnp.bfloat16)


def draw_cache_values(key, part):
    return head_draw(jax.random.fold_in(key, 71), CL).astype(jnp.bfloat16)


def draw_queries(key, part):
    shape = (NTRAJ, TURN, Q_HEADS * HD)
    return jnp.clip(jax.random.normal(jax.random.fold_in(key, 31), shape, jnp.float32), -6.0, 6.0).astype(jnp.bfloat16)


def draw_cache_keys(key, part):
    cached = head_draw(jax.random.fold_in(key, 51), CL)
    return cached.astype(jnp.bfloat16)


def levels(own_key, shape, shards, low, high):
    level = 1.0
    for position, blocks in shards:
        draws = jax.random.uniform(jax.random.fold_in(jax.random.fold_in(own_key, 6), position), (blocks,), jnp.float32, low / len(shards), high / len(shards))
        level = level * jnp.repeat(jnp.exp(draws), shape[position] // blocks).reshape((-1,) + (1,) * (len(shape) - 1 - position))
    return level


def profile(number_of, total, reach, slope):
    portions = [(1 << 20) // math.isqrt(rank ** slope) + 1 for rank in range(2, number_of + 1)]
    spare, given = total - reach - (number_of - 1), [1] * (number_of - 1)
    while spare > 0:
        movable = [i for i in range(number_of - 1) if given[i] < reach]
        whole, left = sum([portions[i] for i in movable]), spare
        for i in movable:
            more = min(reach - given[i], max(1, left * portions[i] // whole), spare)
            given[i] = given[i] + more
            spare = spare - more
    return np.array([reach] + given)


def uneven(rng, amount, total, bound, skew):
    if amount == 2:
        one = jax.random.randint(rng, (), max(1, total - bound), min(bound, total - 1) + 1)
        return jnp.stack([one, total - one])
    lengths = jnp.asarray(profile(amount, total, bound, skew), jnp.int32)
    pairs = (amount - 1) // 2
    giver, taker = lengths[1:1 + 2 * pairs:2], lengths[2:2 + 2 * pairs:2]
    margin = jnp.minimum(giver - 1, bound - taker)
    moved = jax.random.randint(jax.random.fold_in(rng, 1), (pairs,), 0, 1 << 20) % (margin + 1)
    lengths = lengths.at[1:1 + 2 * pairs:2].set(giver - moved).at[2:2 + 2 * pairs:2].set(taker + moved)
    return lengths[jax.random.permutation(jax.random.fold_in(rng, 2), amount)]


def gaussian(own_key, extent, spread, reach, cuts=(), kind=jnp.bfloat16):
    loudness = levels(own_key, extent, cuts, -0.22, 0.18) if cuts else 1.0
    entries = jax.random.normal(own_key, extent, jnp.float32) * spread * loudness
    return jnp.minimum(jnp.maximum(entries, -reach), reach).astype(kind)


def setup_inputs(seed: int = 0) -> dict:
    arg_keys = jax.random.split(jax.random.key(seed), 11)
    return {
        "queries": draw_queries(jax.random.fold_in(arg_keys[10], 71), 0),
        "new_keys": draw_new_keys(jax.random.fold_in(arg_keys[10], 71), 0),
        "new_values": draw_new_values(jax.random.fold_in(arg_keys[10], 71), 0),
        "cache_keys": draw_cache_keys(jax.random.fold_in(arg_keys[10], 71), 0),
        "cache_values": draw_cache_values(jax.random.fold_in(arg_keys[10], 71), 0),
        "serve_lists": draw_serve_lists(jax.random.fold_in(arg_keys[10], 71), 0),
        "turn_lens": uneven(arg_keys[6], NTRAJ, NTRAJ * TURN // 2 + NTRAJ // 2, TURN, 2).astype(jnp.int32),
        "cache_lens": uneven(arg_keys[7], NTRAJ, NTRAJ * CL // 2, CL, 1).astype(jnp.int32),
        "owner_map": jax.random.permutation(arg_keys[8], N_REPLICA).astype(jnp.int32),
        "new_wo": gaussian(arg_keys[9], (N_REPLICA, Q_HEADS * HD // N_REPLICA, D), (Q_HEADS * HD) ** -0.5, 0.0625, ((0, 32), (1, 16))),
    }


def attend(query_rows, key_rows, value_rows, cache_k, cache_v, live_turn, live_cache):
    slot_count, turn_size, query_cols = query_rows.shape
    cache_size = cache_k.shape[1]
    key_blocks = key_rows.shape[2] // HD
    group_size = query_cols // HD // key_blocks
    all_keys = jnp.concatenate([cache_k, key_rows], axis=1).reshape(slot_count, cache_size + turn_size, key_blocks, HD)
    all_values = jnp.concatenate([cache_v, value_rows], axis=1).reshape(slot_count, cache_size + turn_size, key_blocks, HD)
    grouped = query_rows.reshape(slot_count, turn_size, key_blocks, group_size, HD)
    scores = jnp.einsum('bpkgd,bckd->bkgpc', grouped.astype(jnp.float32), all_keys.astype(jnp.float32)) / math.sqrt(HD)
    positions = jnp.arange(cache_size + turn_size, dtype=jnp.int32)
    query_pos = jnp.arange(turn_size, dtype=jnp.int32)
    allowed = jnp.where(positions[None, None, :] < cache_size, positions[None, None, :] < live_cache[:, None, None], positions[None, None, :] - cache_size <= query_pos[None, :, None])
    scores = jnp.where(allowed[:, None, None, :, :], scores, -jnp.inf)
    row_max = lax.optimization_barrier(jnp.max(scores, axis=-1, keepdims=True))
    exponent = jnp.exp(scores - row_max)
    soft_weights = (exponent / lax.optimization_barrier(jnp.sum(exponent, axis=-1, keepdims=True))).astype(jnp.bfloat16)
    mixed_values = jnp.einsum('bkgpc,bckd->bpkgd', soft_weights.astype(jnp.float32), all_values.astype(jnp.float32))
    live_rows = query_pos[None, :] < live_turn[:, None]
    mixed_values = jnp.where(live_rows[:, :, None, None, None], mixed_values, 0.0)
    return mixed_values.astype(jnp.bfloat16).reshape(slot_count, turn_size, query_cols)

def reference(queries, new_keys, new_values, cache_keys, cache_values, serve_lists, turn_lens, cache_lens, owner_map, new_wo):
    replica_count = N_REPLICA
    w_stack = jnp.take(new_wo.reshape(replica_count, N_TENSOR, OWN_ROWS, D), owner_map, axis=0)
    w_stack = jnp.transpose(w_stack, (1, 0, 2, 3)).reshape(N_TENSOR, QH_DEV * HD, D)

    def per_replica(replica_id):
        slot_lists = jnp.take(serve_lists, replica_id, axis=0)
        query_rows = jnp.take(queries, slot_lists, axis=0)
        key_rows = jnp.take(new_keys, slot_lists, axis=0)
        value_rows = jnp.take(new_values, slot_lists, axis=0)
        first_slot = (replica_id * replica_count).astype(jnp.int32)
        cache_k = lax.dynamic_slice_in_dim(cache_keys, first_slot, replica_count, 0)
        cache_v = lax.dynamic_slice_in_dim(cache_values, first_slot, replica_count, 0)
        live_cache = lax.dynamic_slice_in_dim(cache_lens, first_slot, replica_count, 0)
        live_turn = jnp.take(turn_lens, slot_lists)
        attended = attend(query_rows, key_rows, value_rows, cache_k, cache_v, live_turn, live_cache)
        attended = attended.reshape(replica_count * TURN, N_TENSOR, QH_DEV * HD)
        partial_value = jnp.einsum('rtc,tcd->trd', attended.astype(jnp.float32), w_stack.astype(jnp.float32))
        partial_value = lax.optimization_barrier(partial_value.astype(jnp.bfloat16))
        return lax.optimization_barrier(jnp.sum(partial_value.astype(jnp.float32), axis=0)).astype(jnp.bfloat16)
    return lax.map(per_replica, jnp.arange(replica_count, dtype=jnp.int32))
```

```python
import functools
import math

import jax
import jax.numpy as jnp
from jax import lax
from jax.experimental import pallas as pl
from jax.experimental.pallas import tpu as pltpu
from jax.sharding import Mesh
from jax.sharding import PartitionSpec as P

HD = 128
TURN = 4
HEADS = 4
OWN = 16
REPL = ("z_lo", "y", "core")
TENS = ("z_hi", "x")
NREP = 32
NCOL = 8
SLOTS = 32
QROWS = HEADS * TURN
VM = pl.BlockSpec(memory_space=pltpu.VMEM)
SM = pl.BlockSpec(memory_space=pltpu.SMEM)


def pack_kernel(index_ref, q_ref, k_ref, v_ref, w_ref, out_ref):
    blocks = w_ref.shape[2] // NCOL // HD
    for part in range(NCOL):
        for j in range(blocks):
            first = (part * blocks + j) * HD
            piece = w_ref[0, :, first : first + HD]
            for far in range(NREP // NCOL):
                out_ref[far * NCOL + part, j * OWN : (j + 1) * OWN, :] = piece
    base = blocks * OWN
    for r in range(NREP):
        i = index_ref[r]
        rows = q_ref[i]
        for h in range(HEADS):
            out_ref[r, base + h * TURN : base + (h + 1) * TURN, :] = rows[:, h * HD : (h + 1) * HD]
        out_ref[r, base + QROWS : base + QROWS + TURN, :] = k_ref[i]
        out_ref[r, base + QROWS + TURN : base + QROWS + 2 * TURN, :] = v_ref[i]


def attend_kernel(base, own_ref, serve_ref, turn_ref, cache_ref, got_ref, ck_ref, cv_ref, out_ref, nk, nv, s1, acc):
    own = own_ref[0]
    rows = SLOTS * QROWS
    scale = 1.0 / math.sqrt(HD)
    lane = lax.broadcasted_iota(jnp.int32, (QROWS, HD), 1)
    turn_pos = lax.broadcasted_iota(jnp.int32, (QROWS, HD), 0) % TURN
    queries = []
    for s in range(SLOTS):
        source = serve_ref[own, s] // NREP
        queries.append(got_ref[source, base : base + QROWS, :])
        nk[s * TURN : (s + 1) * TURN, :] = got_ref[source, base + QROWS : base + QROWS + TURN, :]
        nv[s * TURN : (s + 1) * TURN, :] = got_ref[source, base + QROWS + TURN : base + QROWS + 2 * TURN, :]
        raw = lax.dot_general(queries[s], ck_ref[s], (((1,), (1,)), ((), ())), preferred_element_type=jnp.float32)
        s1[s * QROWS : (s + 1) * QROWS, :] = jnp.where(lane < cache_ref[s], raw * scale, -jnp.inf)
    all_q = jnp.concatenate(queries, axis=0)
    fresh = lax.dot_general(all_q, nk[...], (((1,), (1,)), ((), ())), preferred_element_type=jnp.float32)
    row = lax.broadcasted_iota(jnp.int32, (rows, SLOTS * TURN), 0)
    col = lax.broadcasted_iota(jnp.int32, (rows, SLOTS * TURN), 1)
    seen = (col // TURN == row // QROWS) & (col % TURN <= row % TURN)
    fresh = jnp.where(seen, fresh * scale, -jnp.inf)
    cached = s1[...]
    top = jnp.max(jnp.maximum(cached, fresh), axis=1, keepdims=True)
    e1 = jnp.exp(cached - top)
    e2 = jnp.exp(fresh - top)
    total = jnp.sum(e1 + e2, axis=1, keepdims=True)
    w1 = (e1 / total).astype(jnp.bfloat16)
    w2 = (e2 / total).astype(jnp.bfloat16)
    acc[...] = jnp.dot(w2, nv[...], preferred_element_type=jnp.float32)
    for s in range(SLOTS):
        part = slice(s * QROWS, (s + 1) * QROWS)
        mixed = acc[part, :] + jnp.dot(w1[part, :], cv_ref[s], preferred_element_type=jnp.float32)
        live = turn_ref[serve_ref[own, s]]
        mixed = jnp.where(turn_pos < live, mixed, 0.0).astype(jnp.bfloat16)
        t = s // 2
        z, x, at = t // 4, t % 4, (s % 2) * TURN
        for h in range(HEADS):
            out_ref[x, z, at : at + TURN, h * HD : (h + 1) * HD] = mixed[h * TURN : (h + 1) * TURN, :]


def weight_kernel(owner_ref, got_ref, out_ref):
    for b in range(NREP):
        source = owner_ref[b]
        for j in range(out_ref.shape[1] // HD):
            out_ref[b * OWN : (b + 1) * OWN, j * HD : (j + 1) * HD] = got_ref[source, j * OWN : (j + 1) * OWN, :]


def matmul_kernel(rows_ref, w_ref, out_ref):
    for x in range(out_ref.shape[0]):
        block = rows_ref[:, x].reshape(out_ref.shape[1], rows_ref.shape[-1])
        out_ref[x] = jnp.dot(block, w_ref[...], preferred_element_type=jnp.float32).astype(jnp.bfloat16)


def on_device(
    queries,
    new_keys,
    new_values,
    cache_keys,
    cache_values,
    serve_lists,
    turn_lens,
    cache_lens,
    owner_map,
    new_wo,
):
    own = lax.axis_index(REPL)
    out_width = new_wo.shape[2]
    width = out_width // NCOL
    base = width // HD * OWN
    sources = serve_lists // NREP
    send_index = jnp.sum(jnp.where(sources == own, serve_lists % NREP, 0), axis=1)
    packed = pl.pallas_call(
        pack_kernel,
        out_shape=jax.ShapeDtypeStruct((NREP, base + QROWS + 2 * TURN, HD), jnp.bfloat16),
        in_specs=[SM, VM, VM, VM, VM],
        out_specs=VM,
    )(send_index, queries, new_keys, new_values, new_wo)
    got = lax.all_to_all(packed, REPL, split_axis=0, concat_axis=0, tiled=True)
    attended = pl.pallas_call(
        functools.partial(attend_kernel, base),
        out_shape=jax.ShapeDtypeStruct((4, 4, 2 * TURN, HEADS * HD), jnp.bfloat16),
        in_specs=[SM, SM, SM, SM, VM, VM, VM],
        out_specs=VM,
        scratch_shapes=[
            pltpu.VMEM((SLOTS * TURN, HD), jnp.bfloat16),
            pltpu.VMEM((SLOTS * TURN, HD), jnp.bfloat16),
            pltpu.VMEM((SLOTS * QROWS, HD), jnp.float32),
            pltpu.VMEM((SLOTS * QROWS, HD), jnp.float32),
        ],
    )(own.reshape(1), serve_lists, turn_lens, cache_lens, got, cache_keys, cache_values)
    copies = jnp.broadcast_to(attended[None], (NCOL,) + attended.shape)
    rows = lax.all_to_all(copies, ("y", "core"), split_axis=0, concat_axis=0, tiled=True)
    weight = pl.pallas_call(
        weight_kernel,
        out_shape=jax.ShapeDtypeStruct((NREP * OWN, width), jnp.bfloat16),
        in_specs=[SM, VM],
        out_specs=VM,
        cost_estimate=pl.CostEstimate(flops=0, bytes_accessed=2 * 2 * NREP * OWN * width, transcendentals=0),
    )(owner_map, got)
    partial = pl.pallas_call(
        matmul_kernel,
        out_shape=jax.ShapeDtypeStruct((4, NCOL * 4 * 2 * TURN, width), jnp.bfloat16),
        in_specs=[VM, VM],
        out_specs=VM,
    )(rows, weight)
    over_x = lax.all_to_all(partial, "x", split_axis=0, concat_axis=0, tiled=True)
    summed = jnp.sum(over_x.astype(jnp.float32), axis=0).astype(jnp.bfloat16)
    summed = summed.reshape(NCOL * 4, 2 * TURN, width)
    over_z = lax.all_to_all(summed, ("y", "core", "z_hi"), split_axis=0, concat_axis=0, tiled=True)
    over_z = over_z.reshape(NCOL, 4, 2 * TURN, width)
    projected = jnp.sum(over_z.astype(jnp.float32), axis=1).astype(jnp.bfloat16)
    return jnp.transpose(projected, (1, 0, 2)).reshape(1, 2 * TURN, out_width)


def solution(mesh):
    fine = Mesh(mesh.devices.reshape(4, 4, 2, 4, 4), REPL + TENS)
    placed = (
        P(REPL, None, TENS),
        P(REPL, None, TENS),
        P(REPL, None, TENS),
        P(REPL, None, TENS),
        P(REPL, None, TENS),
        P(),
        P(),
        P(REPL),
        P(),
        P(REPL, TENS, None),
    )
    return jax.shard_map(
        on_device,
        mesh=fine,
        in_specs=placed,
        out_specs=P(REPL, TENS, None),
        check_vma=False,
    )
```

```python
import math

import jax
import jax.numpy as jnp
from jax import lax
from jax.experimental import pallas as pl
from jax.experimental.pallas import tpu as pltpu
from jax.sharding import Mesh
from jax.sharding import PartitionSpec as P

HD = 128
TURN = 4
HEADS = 4
OWN = 16
REPL = ("z_lo", "y", "core")
TENS = ("z_hi", "x")
NREP = 32
NCOL = 8
SLOTS = 32
QROWS = HEADS * TURN
VM = pl.BlockSpec(memory_space=pltpu.VMEM)
SM = pl.BlockSpec(memory_space=pltpu.SMEM)
ROOM = pltpu.CompilerParams(vmem_limit_bytes=16 << 20)


def route_kernel(index_ref, q_ref, k_ref, v_ref, out_ref):
    for r in range(NREP):
        i = index_ref[r]
        rows = q_ref[i]
        for h in range(HEADS):
            out_ref[r, h * TURN : (h + 1) * TURN, :] = rows[:, h * HD : (h + 1) * HD]
        out_ref[r, QROWS : QROWS + TURN, :] = k_ref[i]
        out_ref[r, QROWS + TURN : QROWS + 2 * TURN, :] = v_ref[i]


def spread_kernel(w_ref, out_ref):
    blocks = w_ref.shape[2] // NCOL // HD
    for part in range(NCOL):
        for j in range(blocks):
            first = (part * blocks + j) * HD
            piece = w_ref[0, :, first : first + HD]
            for far in range(NREP // NCOL):
                out_ref[far * NCOL + part, j * OWN : (j + 1) * OWN, :] = piece


def attend_kernel(own_ref, serve_ref, turn_ref, cache_ref, got_ref, ck_ref, cv_ref, out_ref, nk, nv, s1, acc):
    own = own_ref[0]
    rows = SLOTS * QROWS
    scale = 1.0 / math.sqrt(HD)
    lane = lax.broadcasted_iota(jnp.int32, (QROWS, HD), 1)
    turn_pos = lax.broadcasted_iota(jnp.int32, (QROWS, HD), 0) % TURN
    queries = []
    for s in range(SLOTS):
        source = serve_ref[own, s] // NREP
        queries.append(got_ref[source, 0:QROWS, :])
        nk[s * TURN : (s + 1) * TURN, :] = got_ref[source, QROWS : QROWS + TURN, :]
        nv[s * TURN : (s + 1) * TURN, :] = got_ref[source, QROWS + TURN : QROWS + 2 * TURN, :]
        raw = lax.dot_general(queries[s], ck_ref[s], (((1,), (1,)), ((), ())), preferred_element_type=jnp.float32)
        s1[s * QROWS : (s + 1) * QROWS, :] = jnp.where(lane < cache_ref[s], raw * scale, -jnp.inf)
    all_q = jnp.concatenate(queries, axis=0)
    fresh = lax.dot_general(all_q, nk[...], (((1,), (1,)), ((), ())), preferred_element_type=jnp.float32)
    row = lax.broadcasted_iota(jnp.int32, (rows, SLOTS * TURN), 0)
    col = lax.broadcasted_iota(jnp.int32, (rows, SLOTS * TURN), 1)
    seen = (col // TURN == row // QROWS) & (col % TURN <= row % TURN)
    fresh = jnp.where(seen, fresh * scale, -jnp.inf)
    cached = s1[...]
    top = jnp.max(jnp.maximum(cached, fresh), axis=1, keepdims=True)
    e1 = jnp.exp(cached - top)
    e2 = jnp.exp(fresh - top)
    total = jnp.sum(e1 + e2, axis=1, keepdims=True)
    w1 = (e1 / total).astype(jnp.bfloat16)
    w2 = (e2 / total).astype(jnp.bfloat16)
    acc[...] = jnp.dot(w2, nv[...], preferred_element_type=jnp.float32)
    for s in range(SLOTS):
        part = slice(s * QROWS, (s + 1) * QROWS)
        mixed = acc[part, :] + jnp.dot(w1[part, :], cv_ref[s], preferred_element_type=jnp.float32)
        live = turn_ref[serve_ref[own, s]]
        mixed = jnp.where(turn_pos < live, mixed, 0.0).astype(jnp.bfloat16)
        t = s // 2
        z, x, at = t // 4, t % 4, (s % 2) * TURN
        for h in range(HEADS):
            out_ref[x, z, at : at + TURN, h * HD : (h + 1) * HD] = mixed[h * TURN : (h + 1) * TURN, :]


def weight_kernel(owner_ref, got_ref, out_ref):
    for b in range(NREP):
        source = owner_ref[b]
        for j in range(out_ref.shape[1] // HD):
            out_ref[b * OWN : (b + 1) * OWN, j * HD : (j + 1) * HD] = got_ref[source, j * OWN : (j + 1) * OWN, :]


def matmul_kernel(core_ref, near_ref, far_ref, w_ref, out_ref, rows):
    core = core_ref[0]
    for y in range(4):
        rows[y, core] = near_ref[y, 0]
        rows[y, 1 - core] = far_ref[y, 0]
    block = rows[...].reshape(out_ref.shape[1], rows.shape[-1])
    out_ref[0] = jnp.dot(block, w_ref[...], preferred_element_type=jnp.float32).astype(jnp.bfloat16)


def on_device(
    queries,
    new_keys,
    new_values,
    cache_keys,
    cache_values,
    serve_lists,
    turn_lens,
    cache_lens,
    owner_map,
    new_wo,
):
    own = lax.axis_index(REPL)
    out_width = new_wo.shape[2]
    width = out_width // NCOL
    sources = serve_lists // NREP
    send_index = jnp.sum(jnp.where(sources == own, serve_lists % NREP, 0), axis=1)
    routed = pl.pallas_call(
        route_kernel,
        out_shape=jax.ShapeDtypeStruct((NREP, QROWS + 2 * TURN, HD), jnp.bfloat16),
        compiler_params=ROOM,
        in_specs=[SM, VM, VM, VM],
        out_specs=VM,
    )(send_index, queries, new_keys, new_values)
    spread = pl.pallas_call(
        spread_kernel,
        out_shape=jax.ShapeDtypeStruct((NREP, width // HD * OWN, HD), jnp.bfloat16),
        compiler_params=ROOM,
        in_specs=[VM],
        out_specs=VM,
    )(new_wo)
    got = lax.all_to_all(routed, REPL, split_axis=0, concat_axis=0, tiled=True)
    got, spread = lax.optimization_barrier((got, spread))
    pieces = lax.all_to_all(spread, REPL, split_axis=0, concat_axis=0, tiled=True)
    attended = pl.pallas_call(
        attend_kernel,
        out_shape=jax.ShapeDtypeStruct((4, 4, 2 * TURN, HEADS * HD), jnp.bfloat16),
        compiler_params=ROOM,
        in_specs=[SM, SM, SM, SM, VM, VM, VM],
        out_specs=VM,
        scratch_shapes=[
            pltpu.VMEM((SLOTS * TURN, HD), jnp.bfloat16),
            pltpu.VMEM((SLOTS * TURN, HD), jnp.bfloat16),
            pltpu.VMEM((SLOTS * QROWS, HD), jnp.float32),
            pltpu.VMEM((SLOTS * QROWS, HD), jnp.float32),
        ],
        cost_estimate=pl.CostEstimate(flops=1 << 30, bytes_accessed=8 << 20, transcendentals=1 << 17),
    )(own.reshape(1), serve_lists, turn_lens, cache_lens, got, cache_keys, cache_values)
    near = lax.all_gather(attended, "y", axis=0)
    far = lax.ppermute(near, "core", [(0, 1), (1, 0)])
    weight = pl.pallas_call(
        weight_kernel,
        out_shape=jax.ShapeDtypeStruct((NREP * OWN, width), jnp.bfloat16),
        compiler_params=ROOM,
        in_specs=[SM, VM],
        out_specs=VM,
        cost_estimate=pl.CostEstimate(flops=0, bytes_accessed=2 * 2 * NREP * OWN * width, transcendentals=0),
    )(owner_map, pieces)
    block = (4, 1, 4, 2 * TURN, HEADS * HD)
    partial = pl.pallas_call(
        matmul_kernel,
        out_shape=jax.ShapeDtypeStruct((4, NCOL * 4 * 2 * TURN, width), jnp.bfloat16),
        grid=(4,),
        compiler_params=ROOM,
        in_specs=[
            SM,
            pl.BlockSpec(block, lambda x: (0, x, 0, 0, 0)),
            pl.BlockSpec(block, lambda x: (0, x, 0, 0, 0)),
            pl.BlockSpec((NREP * OWN, width), lambda x: (0, 0)),
        ],
        out_specs=pl.BlockSpec((1, NCOL * 4 * 2 * TURN, width), lambda x: (x, 0, 0)),
        scratch_shapes=[pltpu.VMEM((4, 2, 4, 2 * TURN, HEADS * HD), jnp.bfloat16)],
    )(lax.axis_index("core").reshape(1), near, far, weight)
    over_x = lax.all_to_all(partial, "x", split_axis=0, concat_axis=0, tiled=True)
    summed = jnp.sum(over_x.astype(jnp.float32), axis=0).astype(jnp.bfloat16)
    summed = summed.reshape(NCOL * 4, 2 * TURN, width)
    over_z = lax.all_to_all(summed, ("y", "core", "z_hi"), split_axis=0, concat_axis=0, tiled=True)
    over_z = over_z.reshape(NCOL, 4, 2 * TURN, width)
    projected = jnp.sum(over_z.astype(jnp.float32), axis=1).astype(jnp.bfloat16)
    return jnp.transpose(projected, (1, 0, 2)).reshape(1, 2 * TURN, out_width)


def solution(mesh):
    fine = Mesh(mesh.devices.reshape(4, 4, 2, 4, 4), REPL + TENS)
    placed = (
        P(REPL, None, TENS),
        P(REPL, None, TENS),
        P(REPL, None, TENS),
        P(REPL, None, TENS),
        P(REPL, None, TENS),
        P(),
        P(),
        P(REPL),
        P(),
        P(REPL, TENS, None),
    )
    return jax.shard_map(
        on_device,
        mesh=fine,
        in_specs=placed,
        out_specs=P(REPL, TENS, None),
        check_vma=False,
    )
```

```python
import math

import jax
import jax.numpy as jnp
from jax import lax
from jax.experimental import pallas as pl
from jax.experimental.pallas import tpu as pltpu
from jax.sharding import Mesh
from jax.sharding import PartitionSpec as P

HD = 128
TURN = 4
HEADS = 4
OWN = 16
REPL = ("z_lo", "y", "core")
TENS = ("z_hi", "x")
NREP = 32
NCOL = 8
SLOTS = 32
QROWS = HEADS * TURN
VM = pl.BlockSpec(memory_space=pltpu.VMEM)
SM = pl.BlockSpec(memory_space=pltpu.SMEM)
ROOM = pltpu.CompilerParams(vmem_limit_bytes=16 << 20)


def route_kernel(index_ref, q_ref, k_ref, v_ref, out_ref):
    for r in range(NREP):
        i = index_ref[r]
        rows = q_ref[i]
        for h in range(HEADS):
            out_ref[r, h * TURN : (h + 1) * TURN, :] = rows[:, h * HD : (h + 1) * HD]
        out_ref[r, QROWS : QROWS + TURN, :] = k_ref[i]
        out_ref[r, QROWS + TURN : QROWS + 2 * TURN, :] = v_ref[i]


def spread_kernel(w_ref, out_ref):
    blocks = w_ref.shape[2] // NCOL // HD
    for part in range(NCOL):
        for j in range(blocks):
            first = (part * blocks + j) * HD
            piece = w_ref[0, :, first : first + HD]
            for far in range(NREP // NCOL):
                out_ref[far * NCOL + part, j * OWN : (j + 1) * OWN, :] = piece


def attend_kernel(own_ref, serve_ref, turn_ref, cache_ref, got_ref, ck_ref, cv_ref, out_ref, nk, nv, s1, acc):
    own = own_ref[0]
    rows = SLOTS * QROWS
    scale = 1.0 / math.sqrt(HD)
    lane = lax.broadcasted_iota(jnp.int32, (QROWS, HD), 1)
    turn_pos = lax.broadcasted_iota(jnp.int32, (QROWS, HD), 0) % TURN
    queries = []
    for s in range(SLOTS):
        source = serve_ref[own, s] // NREP
        queries.append(got_ref[source, 0:QROWS, :])
        nk[s * TURN : (s + 1) * TURN, :] = got_ref[source, QROWS : QROWS + TURN, :]
        nv[s * TURN : (s + 1) * TURN, :] = got_ref[source, QROWS + TURN : QROWS + 2 * TURN, :]
        raw = lax.dot_general(queries[s], ck_ref[s], (((1,), (1,)), ((), ())), preferred_element_type=jnp.float32)
        s1[s * QROWS : (s + 1) * QROWS, :] = jnp.where(lane < cache_ref[s], raw * scale, -jnp.inf)
    all_q = jnp.concatenate(queries, axis=0)
    fresh = lax.dot_general(all_q, nk[...], (((1,), (1,)), ((), ())), preferred_element_type=jnp.float32)
    row = lax.broadcasted_iota(jnp.int32, (rows, SLOTS * TURN), 0)
    col = lax.broadcasted_iota(jnp.int32, (rows, SLOTS * TURN), 1)
    seen = (col // TURN == row // QROWS) & (col % TURN <= row % TURN)
    fresh = jnp.where(seen, fresh * scale, -jnp.inf)
    cached = s1[...]
    top = jnp.max(jnp.maximum(cached, fresh), axis=1, keepdims=True)
    e1 = jnp.exp(cached - top)
    e2 = jnp.exp(fresh - top)
    total = jnp.sum(e1 + e2, axis=1, keepdims=True)
    w1 = (e1 / total).astype(jnp.bfloat16)
    w2 = (e2 / total).astype(jnp.bfloat16)
    acc[...] = jnp.dot(w2, nv[...], preferred_element_type=jnp.float32)
    for s in range(SLOTS):
        part = slice(s * QROWS, (s + 1) * QROWS)
        mixed = acc[part, :] + jnp.dot(w1[part, :], cv_ref[s], preferred_element_type=jnp.float32)
        live = turn_ref[serve_ref[own, s]]
        mixed = jnp.where(turn_pos < live, mixed, 0.0).astype(jnp.bfloat16)
        t = s // 2
        z, x, at = t // 4, t % 4, (s % 2) * TURN
        for h in range(HEADS):
            out_ref[x, z, at : at + TURN, h * HD : (h + 1) * HD] = mixed[h * TURN : (h + 1) * TURN, :]


def weight_kernel(owner_ref, got_ref, out_ref):
    for b in range(NREP):
        source = owner_ref[b]
        for j in range(out_ref.shape[1] // HD):
            out_ref[b * OWN : (b + 1) * OWN, j * HD : (j + 1) * HD] = got_ref[source, j * OWN : (j + 1) * OWN, :]


def matmul_kernel(core_ref, near_ref, far_ref, w_ref, out_ref, rows):
    core = core_ref[0]
    rows[core] = near_ref[0]
    rows[1 - core] = far_ref[0]
    block = rows[...].reshape(2 * rows.shape[1], rows.shape[2])
    product = jnp.dot(block, w_ref[...], preferred_element_type=jnp.float32).astype(jnp.bfloat16)
    out_ref[0] = product.reshape(out_ref.shape[1:])


def on_device(
    queries,
    new_keys,
    new_values,
    cache_keys,
    cache_values,
    serve_lists,
    turn_lens,
    cache_lens,
    owner_map,
    new_wo,
):
    own = lax.axis_index(REPL)
    out_width = new_wo.shape[2]
    width = out_width // NCOL
    sources = serve_lists // NREP
    send_index = jnp.sum(jnp.where(sources == own, serve_lists % NREP, 0), axis=1)
    routed = pl.pallas_call(
        route_kernel,
        out_shape=jax.ShapeDtypeStruct((NREP, QROWS + 2 * TURN, HD), jnp.bfloat16),
        in_specs=[SM, VM, VM, VM],
        out_specs=VM,
    )(send_index, queries, new_keys, new_values)
    spread = pl.pallas_call(
        spread_kernel,
        out_shape=jax.ShapeDtypeStruct((NREP, width // HD * OWN, HD), jnp.bfloat16),
        compiler_params=ROOM,
        in_specs=[VM],
        out_specs=VM,
    )(new_wo)
    got = lax.all_to_all(routed, REPL, split_axis=0, concat_axis=0, tiled=True)
    got, spread = lax.optimization_barrier((got, spread))
    pieces = lax.all_to_all(spread, REPL, split_axis=0, concat_axis=0, tiled=True)
    attended = pl.pallas_call(
        attend_kernel,
        out_shape=jax.ShapeDtypeStruct((4, 4, 2 * TURN, HEADS * HD), jnp.bfloat16),
        compiler_params=ROOM,
        in_specs=[SM, SM, SM, SM, VM, VM, VM],
        out_specs=VM,
        scratch_shapes=[
            pltpu.VMEM((SLOTS * TURN, HD), jnp.bfloat16),
            pltpu.VMEM((SLOTS * TURN, HD), jnp.bfloat16),
            pltpu.VMEM((SLOTS * QROWS, HD), jnp.float32),
            pltpu.VMEM((SLOTS * QROWS, HD), jnp.float32),
        ],
        cost_estimate=pl.CostEstimate(flops=1 << 30, bytes_accessed=8 << 20, transcendentals=1 << 17),
    )(own.reshape(1), serve_lists, turn_lens, cache_lens, got, cache_keys, cache_values)
    near = lax.all_gather(attended, "y", axis=0)
    far = lax.ppermute(near, "core", [(0, 1), (1, 0)])
    weight = pl.pallas_call(
        weight_kernel,
        out_shape=jax.ShapeDtypeStruct((NREP * OWN, width), jnp.bfloat16),
        compiler_params=ROOM,
        in_specs=[SM, VM],
        out_specs=VM,
        cost_estimate=pl.CostEstimate(flops=0, bytes_accessed=2 * 2 * NREP * OWN * width, transcendentals=0),
    )(owner_map, pieces)
    served = SLOTS * TURN
    block = pl.BlockSpec((1, served, HEADS * HD), lambda y: (y, 0, 0))
    partial = pl.pallas_call(
        matmul_kernel,
        out_shape=jax.ShapeDtypeStruct((4, 2, served, width), jnp.bfloat16),
        grid=(4,),
        compiler_params=ROOM,
        in_specs=[SM, block, block, pl.BlockSpec((NREP * OWN, width), lambda y: (0, 0))],
        out_specs=pl.BlockSpec((1, 2, served, width), lambda y: (y, 0, 0, 0)),
        scratch_shapes=[pltpu.VMEM((2, served, HEADS * HD), jnp.bfloat16)],
    )(
        lax.axis_index("core").reshape(1),
        near.reshape(4, served, HEADS * HD),
        far.reshape(4, served, HEADS * HD),
        weight,
    )
    partial = partial.reshape(NREP, NREP, width)
    over_x = lax.all_to_all(partial, ("y", "core", "x"), split_axis=0, concat_axis=0, tiled=True)
    summed = jnp.sum(over_x.reshape(NCOL, 4, 4, 2 * TURN, width).astype(jnp.float32), axis=1)
    summed = jnp.transpose(summed.astype(jnp.bfloat16), (1, 0, 2, 3))
    over_z = lax.all_to_all(summed, "z_hi", split_axis=0, concat_axis=0, tiled=True)
    projected = jnp.sum(over_z.astype(jnp.float32), axis=0).astype(jnp.bfloat16)
    return jnp.transpose(projected, (1, 0, 2)).reshape(1, 2 * TURN, out_width)


def solution(mesh):
    fine = Mesh(mesh.devices.reshape(4, 4, 2, 4, 4), REPL + TENS)
    placed = (
        P(REPL, None, TENS),
        P(REPL, None, TENS),
        P(REPL, None, TENS),
        P(REPL, None, TENS),
        P(REPL, None, TENS),
        P(),
        P(),
        P(REPL),
        P(),
        P(REPL, TENS, None),
    )
    return jax.shard_map(
        on_device,
        mesh=fine,
        in_specs=placed,
        out_specs=P(REPL, TENS, None),
        check_vma=False,
    )
```

```python
import math

import jax
import jax.numpy as jnp
from jax import lax
from jax.experimental import pallas as pl
from jax.experimental.pallas import tpu as pltpu
from jax.sharding import Mesh
from jax.sharding import PartitionSpec as P

HD = 128
TURN = 4
HEADS = 4
OWN = 16
REPL = ("z_lo", "y", "core")
TENS = ("z_hi", "x")
NREP = 32
NCOL = 8
SLOTS = 32
QROWS = HEADS * TURN
VM = pl.BlockSpec(memory_space=pltpu.VMEM)
SM = pl.BlockSpec(memory_space=pltpu.SMEM)
HBM = pl.BlockSpec(memory_space=pltpu.HBM)
ROOM = pltpu.CompilerParams(vmem_limit_bytes=16 << 20)


def route_kernel(own_ref, serve_hbm, q_hbm, k_hbm, v_hbm, out_ref, serve_ref, q_ref, k_ref, v_ref, sems):
    pairs = ((serve_hbm, serve_ref), (q_hbm, q_ref), (k_hbm, k_ref), (v_hbm, v_ref))
    copies = [pltpu.make_async_copy(src, dst, sems.at[n]) for n, (src, dst) in enumerate(pairs)]
    for copy in copies:
        copy.start()
    copies[0].wait()
    serve = serve_ref[...]
    chosen = jnp.where(serve // NREP == own_ref[0], serve % NREP, 0)
    index = [jnp.sum(chosen[r : r + 1, :]) for r in range(NREP)]
    for copy in copies[1:]:
        copy.wait()
    for r in range(NREP):
        i = index[r]
        rows = q_ref[i]
        for h in range(HEADS):
            out_ref[r, h * TURN : (h + 1) * TURN, :] = rows[:, h * HD : (h + 1) * HD]
        out_ref[r, QROWS : QROWS + TURN, :] = k_ref[i]
        out_ref[r, QROWS + TURN : QROWS + 2 * TURN, :] = v_ref[i]


def spread_kernel(core_ref, own_ref, other_ref, out_ref):
    core = core_ref[0]
    blocks = own_ref.shape[2] // NCOL // HD
    for y in range(4):
        for j in range(blocks):
            first = pl.multiple_of(core * (blocks * HD), HD) + (2 * y * blocks + j) * HD
            for w_ref, half in ((own_ref, core), (other_ref, 1 - core)):
                piece = w_ref[0, :, pl.ds(pl.multiple_of(first, HD), HD)]
                for z in range(4):
                    out_ref[z * 4 + y, half, j * OWN : (j + 1) * OWN, :] = piece


def attend_kernel(own_ref, zhi_ref, serve_ref, turn_ref, cache_ref, got_ref, ck_ref, cv_hbm, out_ref, nk, nv, s1, acc, cv_ref, sem):
    values = pltpu.make_async_copy(cv_hbm, cv_ref, sem)
    values.start()
    own = own_ref[0]
    rows = SLOTS * QROWS
    scale = 1.0 / math.sqrt(HD)
    lane = lax.broadcasted_iota(jnp.int32, (QROWS, HD), 1)
    turn_pos = lax.broadcasted_iota(jnp.int32, (QROWS, HD), 0) % TURN
    queries = []
    for s in range(SLOTS):
        source = serve_ref[own, s] // NREP
        queries.append(got_ref[source, 0:QROWS, :])
        nk[s * TURN : (s + 1) * TURN, :] = got_ref[source, QROWS : QROWS + TURN, :]
        nv[s * TURN : (s + 1) * TURN, :] = got_ref[source, QROWS + TURN : QROWS + 2 * TURN, :]
        raw = lax.dot_general(queries[s], ck_ref[s], (((1,), (1,)), ((), ())), preferred_element_type=jnp.float32)
        s1[s * QROWS : (s + 1) * QROWS, :] = jnp.where(lane < cache_ref[s], raw * scale, -jnp.inf)
    all_q = jnp.concatenate(queries, axis=0)
    fresh = lax.dot_general(all_q, nk[...], (((1,), (1,)), ((), ())), preferred_element_type=jnp.float32)
    row = lax.broadcasted_iota(jnp.int32, (rows, SLOTS * TURN), 0)
    col = lax.broadcasted_iota(jnp.int32, (rows, SLOTS * TURN), 1)
    seen = (col // TURN == row // QROWS) & (col % TURN <= row % TURN)
    fresh = jnp.where(seen, fresh * scale, -jnp.inf)
    cached = s1[...]
    top = jnp.max(jnp.maximum(cached, fresh), axis=1, keepdims=True)
    e1 = jnp.exp(cached - top)
    e2 = jnp.exp(fresh - top)
    total = jnp.sum(e1 + e2, axis=1, keepdims=True)
    w1 = (e1 / total).astype(jnp.bfloat16)
    w2 = (e2 / total).astype(jnp.bfloat16)
    values.wait()
    acc[...] = jnp.dot(w2, nv[...], preferred_element_type=jnp.float32)
    for s in range(SLOTS):
        part = slice(s * QROWS, (s + 1) * QROWS)
        mixed = acc[part, :] + jnp.dot(w1[part, :], cv_ref[s], preferred_element_type=jnp.float32)
        live = turn_ref[serve_ref[own, s]]
        mixed = jnp.where(turn_pos < live, mixed, 0.0).astype(jnp.bfloat16)
        t = s // 2
        x, at = t % 4, (s % 2) * TURN
        z = (t // 4 + 4 - zhi_ref[0]) % 4
        for h in range(HEADS):
            out_ref[x, z, at : at + TURN, h * HD : (h + 1) * HD] = mixed[h * TURN : (h + 1) * TURN, :]


def weight_kernel(owner_ref, got_ref, out_ref):
    for b in range(NREP):
        source = owner_ref[b]
        for j in range(out_ref.shape[1] // HD):
            piece = got_ref[source // 2, source % 2, j * OWN : (j + 1) * OWN, :]
            out_ref[b * OWN : (b + 1) * OWN, j * HD : (j + 1) * HD] = piece


def matmul_kernel(core_ref, near_ref, far_ref, w_ref, out_ref, rows):
    core = core_ref[0]
    rows[core] = near_ref[0]
    rows[1 - core] = far_ref[0]
    block = rows[...].reshape(2 * rows.shape[1], rows.shape[2])
    product = jnp.dot(block, w_ref[...], preferred_element_type=jnp.float32).astype(jnp.bfloat16)
    out_ref[0] = product.reshape(out_ref.shape[1:])


def on_device(
    queries,
    new_keys,
    new_values,
    cache_keys,
    cache_values,
    serve_lists,
    turn_lens,
    cache_lens,
    owner_map,
    new_wo,
):
    own = lax.axis_index(REPL)
    out_width = new_wo.shape[2]
    width = out_width // NCOL
    core = lax.axis_index("core").reshape(1)
    routed = pl.pallas_call(
        route_kernel,
        out_shape=jax.ShapeDtypeStruct((NREP, QROWS + 2 * TURN, HD), jnp.bfloat16),
        in_specs=[SM, HBM, HBM, HBM, HBM],
        out_specs=VM,
        scratch_shapes=[
            pltpu.VMEM(serve_lists.shape, jnp.int32),
            pltpu.VMEM(queries.shape, jnp.bfloat16),
            pltpu.VMEM(new_keys.shape, jnp.bfloat16),
            pltpu.VMEM(new_values.shape, jnp.bfloat16),
            pltpu.SemaphoreType.DMA((4,)),
        ],
    )(own.reshape(1), serve_lists, queries, new_keys, new_values)
    routed, shard = lax.optimization_barrier((routed, new_wo))
    other = lax.ppermute(shard, "core", [(0, 1), (1, 0)])
    spread = pl.pallas_call(
        spread_kernel,
        out_shape=jax.ShapeDtypeStruct((NREP // 2, 2, width // HD * OWN, HD), jnp.bfloat16),
        compiler_params=ROOM,
        in_specs=[SM, VM, VM],
        out_specs=VM,
        cost_estimate=pl.CostEstimate(flops=0, bytes_accessed=32 << 20, transcendentals=0),
    )(core, shard, other)
    got = lax.all_to_all(routed, REPL, split_axis=0, concat_axis=0, tiled=True)
    got, spread = lax.optimization_barrier((got, spread))
    pieces = lax.all_to_all(spread, ("z_lo", "y"), split_axis=0, concat_axis=0, tiled=True)
    attended = pl.pallas_call(
        attend_kernel,
        out_shape=jax.ShapeDtypeStruct((4, 4, 2 * TURN, HEADS * HD), jnp.bfloat16),
        compiler_params=ROOM,
        in_specs=[SM, SM, SM, SM, SM, VM, VM, HBM],
        out_specs=VM,
        scratch_shapes=[
            pltpu.VMEM((SLOTS * TURN, HD), jnp.bfloat16),
            pltpu.VMEM((SLOTS * TURN, HD), jnp.bfloat16),
            pltpu.VMEM((SLOTS * QROWS, HD), jnp.float32),
            pltpu.VMEM((SLOTS * QROWS, HD), jnp.float32),
            pltpu.VMEM(cache_values.shape, jnp.bfloat16),
            pltpu.SemaphoreType.DMA,
        ],
        cost_estimate=pl.CostEstimate(flops=1 << 30, bytes_accessed=8 << 20, transcendentals=1 << 17),
    )(own.reshape(1), lax.axis_index("z_hi").reshape(1), serve_lists, turn_lens, cache_lens, got, cache_keys, cache_values)
    near = lax.all_gather(attended, "y", axis=0)
    far = lax.ppermute(near, "core", [(0, 1), (1, 0)])
    weight = pl.pallas_call(
        weight_kernel,
        out_shape=jax.ShapeDtypeStruct((NREP * OWN, width), jnp.bfloat16),
        compiler_params=ROOM,
        in_specs=[SM, VM],
        out_specs=VM,
        cost_estimate=pl.CostEstimate(flops=0, bytes_accessed=2 * 2 * NREP * OWN * width, transcendentals=0),
    )(owner_map, pieces)
    served = SLOTS * TURN
    block = pl.BlockSpec((1, served, HEADS * HD), lambda y: (y, 0, 0))
    partial = pl.pallas_call(
        matmul_kernel,
        out_shape=jax.ShapeDtypeStruct((4, 2, served, width), jnp.bfloat16),
        grid=(4,),
        compiler_params=ROOM,
        in_specs=[SM, block, block, pl.BlockSpec((NREP * OWN, width), lambda y: (0, 0))],
        out_specs=pl.BlockSpec((1, 2, served, width), lambda y: (y, 0, 0, 0)),
        scratch_shapes=[pltpu.VMEM((2, served, HEADS * HD), jnp.bfloat16)],
    )(
        core,
        near.reshape(4, served, HEADS * HD),
        far.reshape(4, served, HEADS * HD),
        weight,
    )
    partial = partial.reshape(NREP, NREP, width)
    over_x = lax.all_to_all(partial, ("y", "core", "x"), split_axis=0, concat_axis=0, tiled=True)
    summed = jnp.sum(over_x.reshape(NCOL, 4, 4, 2 * TURN, width).astype(jnp.float32), axis=1)
    summed = jnp.transpose(summed.astype(jnp.bfloat16), (1, 0, 2, 3))
    hops = [lax.ppermute(summed[d], "z_hi", [(i, (i + d) % 4) for i in range(4)]) for d in (2, 1, 3)]
    projected = sum(part.astype(jnp.float32) for part in [summed[0]] + hops).astype(jnp.bfloat16)
    return jnp.transpose(projected, (1, 0, 2)).reshape(1, 2 * TURN, out_width)


def solution(mesh):
    fine = Mesh(mesh.devices.reshape(4, 4, 2, 4, 4), REPL + TENS)
    placed = (
        P(REPL, None, TENS),
        P(REPL, None, TENS),
        P(REPL, None, TENS),
        P(REPL, None, TENS),
        P(REPL, None, TENS),
        P(),
        P(),
        P(REPL),
        P(),
        P(REPL, TENS, None),
    )
    return jax.shard_map(
        on_device,
        mesh=fine,
        in_specs=placed,
        out_specs=P(REPL, TENS, None),
        check_vma=False,
    )
```

```python
import math

import jax
import jax.numpy as jnp
from jax import lax
from jax.experimental import pallas as pl
from jax.experimental.pallas import tpu as pltpu
from jax.sharding import Mesh
from jax.sharding import PartitionSpec as P

HD = 128
TURN = 4
HEADS = 4
OWN = 16
REPL = ("z_lo", "y", "core")
TENS = ("z_hi", "x")
NREP = 32
NCOL = 4
SLOTS = 32
QROWS = HEADS * TURN
VM = pl.BlockSpec(memory_space=pltpu.VMEM)
SM = pl.BlockSpec(memory_space=pltpu.SMEM)
HBM = pl.BlockSpec(memory_space=pltpu.HBM)
ROOM = pltpu.CompilerParams(vmem_limit_bytes=16 << 20)


def route_kernel(own_ref, serve_hbm, q_hbm, k_hbm, v_hbm, out_ref, serve_ref, q_ref, k_ref, v_ref, sems):
    pairs = ((serve_hbm, serve_ref), (q_hbm, q_ref), (k_hbm, k_ref), (v_hbm, v_ref))
    copies = [pltpu.make_async_copy(src, dst, sems.at[n]) for n, (src, dst) in enumerate(pairs)]
    for copy in copies:
        copy.start()
    copies[0].wait()
    serve = serve_ref[...]
    chosen = jnp.where(serve // NREP == own_ref[0], serve % NREP, 0)
    index = [jnp.sum(chosen[r : r + 1, :]) for r in range(NREP)]
    for copy in copies[1:]:
        copy.wait()
    for r in range(NREP):
        i = index[r]
        rows = q_ref[i]
        for h in range(HEADS):
            out_ref[r, h * TURN : (h + 1) * TURN, :] = rows[:, h * HD : (h + 1) * HD]
        out_ref[r, QROWS : QROWS + TURN, :] = k_ref[i]
        out_ref[r, QROWS + TURN : QROWS + 2 * TURN, :] = v_ref[i]


def spread_kernel(w_ref, out_ref):
    blocks = w_ref.shape[2] // NCOL // HD
    for y in range(NCOL):
        for j in range(blocks):
            first = (y * blocks + j) * HD
            piece = w_ref[0, :, first : first + HD]
            for z in range(4):
                out_ref[z * NCOL + y, j * OWN : (j + 1) * OWN, :] = piece


def attend_kernel(own_ref, zhi_ref, serve_ref, turn_ref, cache_ref, got_ref, ck_ref, cv_ref, out_ref, nk, nv, s1, acc):
    own = own_ref[0]
    rows = SLOTS * QROWS
    scale = 1.0 / math.sqrt(HD)
    lane = lax.broadcasted_iota(jnp.int32, (QROWS, HD), 1)
    turn_pos = lax.broadcasted_iota(jnp.int32, (QROWS, HD), 0) % TURN
    queries = []
    for s in range(SLOTS):
        source = serve_ref[own, s] // NREP
        queries.append(got_ref[source, 0:QROWS, :])
        nk[s * TURN : (s + 1) * TURN, :] = got_ref[source, QROWS : QROWS + TURN, :]
        nv[s * TURN : (s + 1) * TURN, :] = got_ref[source, QROWS + TURN : QROWS + 2 * TURN, :]
        raw = lax.dot_general(queries[s], ck_ref[s], (((1,), (1,)), ((), ())), preferred_element_type=jnp.float32)
        s1[s * QROWS : (s + 1) * QROWS, :] = jnp.where(lane < cache_ref[s], raw * scale, -jnp.inf)
    all_q = jnp.concatenate(queries, axis=0)
    fresh = lax.dot_general(all_q, nk[...], (((1,), (1,)), ((), ())), preferred_element_type=jnp.float32)
    row = lax.broadcasted_iota(jnp.int32, (rows, SLOTS * TURN), 0)
    col = lax.broadcasted_iota(jnp.int32, (rows, SLOTS * TURN), 1)
    seen = (col // TURN == row // QROWS) & (col % TURN <= row % TURN)
    fresh = jnp.where(seen, fresh * scale, -jnp.inf)
    cached = s1[...]
    top = jnp.max(jnp.maximum(cached, fresh), axis=1, keepdims=True)
    e1 = jnp.exp(cached - top)
    e2 = jnp.exp(fresh - top)
    total = jnp.sum(e1 + e2, axis=1, keepdims=True)
    w1 = (e1 / total).astype(jnp.bfloat16)
    w2 = (e2 / total).astype(jnp.bfloat16)
    acc[...] = jnp.dot(w2, nv[...], preferred_element_type=jnp.float32)
    for s in range(SLOTS):
        part = slice(s * QROWS, (s + 1) * QROWS)
        mixed = acc[part, :] + jnp.dot(w1[part, :], cv_ref[s], preferred_element_type=jnp.float32)
        live = turn_ref[serve_ref[own, s]]
        mixed = jnp.where(turn_pos < live, mixed, 0.0).astype(jnp.bfloat16)
        t = s // 2
        x, at = t % 4, (s % 2) * TURN
        z = (t // 4 + 4 - zhi_ref[0]) % 4
        for h in range(HEADS):
            out_ref[x, z, at : at + TURN, h * HD : (h + 1) * HD] = mixed[h * TURN : (h + 1) * TURN, :]


def weight_kernel(owner_ref, core_ref, near_ref, far_ref, out_ref, both):
    core = core_ref[0]
    both[core] = near_ref[...]
    both[1 - core] = far_ref[...]
    for b in range(NREP):
        source = owner_ref[b]
        for j in range(out_ref.shape[1] // HD):
            piece = both[source % 2, source // 2, j * OWN : (j + 1) * OWN, :]
            out_ref[b * OWN : (b + 1) * OWN, j * HD : (j + 1) * HD] = piece


def matmul_kernel(rows_ref, w_ref, out_ref):
    out_ref[...] = jnp.dot(rows_ref[...], w_ref[...], preferred_element_type=jnp.float32).astype(jnp.bfloat16)


def on_device(
    queries,
    new_keys,
    new_values,
    cache_keys,
    cache_values,
    serve_lists,
    turn_lens,
    cache_lens,
    owner_map,
    new_wo,
):
    own = lax.axis_index(REPL)
    out_width = new_wo.shape[2]
    width = out_width // NCOL
    core = lax.axis_index("core").reshape(1)
    routed = pl.pallas_call(
        route_kernel,
        out_shape=jax.ShapeDtypeStruct((NREP, QROWS + 2 * TURN, HD), jnp.bfloat16),
        in_specs=[SM, HBM, HBM, HBM, HBM],
        out_specs=VM,
        scratch_shapes=[
            pltpu.VMEM(serve_lists.shape, jnp.int32),
            pltpu.VMEM(queries.shape, jnp.bfloat16),
            pltpu.VMEM(new_keys.shape, jnp.bfloat16),
            pltpu.VMEM(new_values.shape, jnp.bfloat16),
            pltpu.SemaphoreType.DMA((4,)),
        ],
    )(own.reshape(1), serve_lists, queries, new_keys, new_values)
    pieces_shape = (NREP // 2, width // HD * OWN, HD)
    spread = pl.pallas_call(
        spread_kernel,
        out_shape=jax.ShapeDtypeStruct(pieces_shape, jnp.bfloat16),
        compiler_params=ROOM,
        in_specs=[VM],
        out_specs=VM,
        cost_estimate=pl.CostEstimate(flops=0, bytes_accessed=4 << 20, transcendentals=0),
    )(new_wo)
    got = lax.all_to_all(routed, REPL, split_axis=0, concat_axis=0, tiled=True)
    got, spread = lax.optimization_barrier((got, spread))
    pieces = lax.all_to_all(spread, ("z_lo", "y"), split_axis=0, concat_axis=0, tiled=True)
    attended = pl.pallas_call(
        attend_kernel,
        out_shape=jax.ShapeDtypeStruct((4, 4, 2 * TURN, HEADS * HD), jnp.bfloat16),
        compiler_params=ROOM,
        in_specs=[SM, SM, SM, SM, SM, VM, VM, VM],
        out_specs=VM,
        scratch_shapes=[
            pltpu.VMEM((SLOTS * TURN, HD), jnp.bfloat16),
            pltpu.VMEM((SLOTS * TURN, HD), jnp.bfloat16),
            pltpu.VMEM((SLOTS * QROWS, HD), jnp.float32),
            pltpu.VMEM((SLOTS * QROWS, HD), jnp.float32),
        ],
        cost_estimate=pl.CostEstimate(flops=1 << 30, bytes_accessed=8 << 20, transcendentals=1 << 17),
    )(own.reshape(1), lax.axis_index("z_hi").reshape(1), serve_lists, turn_lens, cache_lens, got, cache_keys, cache_values)
    rows = lax.all_gather(attended, "y", axis=0)
    rows, pieces = lax.optimization_barrier((rows, pieces))
    across = lax.ppermute(pieces, "core", [(0, 1), (1, 0)])
    weight = pl.pallas_call(
        weight_kernel,
        out_shape=jax.ShapeDtypeStruct((NREP * OWN, width), jnp.bfloat16),
        compiler_params=ROOM,
        in_specs=[SM, SM, VM, VM],
        out_specs=VM,
        scratch_shapes=[pltpu.VMEM((2,) + pieces_shape, jnp.bfloat16)],
        cost_estimate=pl.CostEstimate(flops=0, bytes_accessed=2 * 2 * NREP * OWN * width, transcendentals=0),
    )(owner_map, core, pieces, across)
    served = SLOTS * TURN
    partial = pl.pallas_call(
        matmul_kernel,
        out_shape=jax.ShapeDtypeStruct((NCOL * served, width), jnp.bfloat16),
        grid=(NCOL // 2,),
        compiler_params=ROOM,
        in_specs=[
            pl.BlockSpec((2 * served, HEADS * HD), lambda i: (i, 0)),
            pl.BlockSpec((NREP * OWN, width), lambda i: (0, 0)),
        ],
        out_specs=pl.BlockSpec((2 * served, width), lambda i: (i, 0)),
    )(rows.reshape(NCOL * served, HEADS * HD), weight)
    partial = partial.reshape(NCOL * 4, 8 * TURN, width)
    over_x = lax.all_to_all(partial, ("y", "x"), split_axis=0, concat_axis=0, tiled=True)
    summed = jnp.sum(over_x.reshape(NCOL, 4, 4, 2 * TURN, width).astype(jnp.float32), axis=1)
    summed = jnp.transpose(summed.astype(jnp.bfloat16), (1, 0, 2, 3))
    hops = [lax.ppermute(summed[d], "z_hi", [(i, (i + d) % 4) for i in range(4)]) for d in (2, 1, 3)]
    projected = sum(part.astype(jnp.float32) for part in [summed[0]] + hops).astype(jnp.bfloat16)
    return jnp.transpose(projected, (1, 0, 2)).reshape(1, 2 * TURN, out_width)


def solution(mesh):
    fine = Mesh(mesh.devices.reshape(4, 4, 2, 4, 4), REPL + TENS)
    placed = (
        P(REPL, None, TENS),
        P(REPL, None, TENS),
        P(REPL, None, TENS),
        P(REPL, None, TENS),
        P(REPL, None, TENS),
        P(),
        P(),
        P(REPL),
        P(),
        P(REPL, TENS, None),
    )
    return jax.shard_map(
        on_device,
        mesh=fine,
        in_specs=placed,
        out_specs=P(REPL, TENS, None),
        check_vma=False,
    )
```

```python
import math

import jax
import jax.numpy as jnp
from jax import lax
from jax.experimental import pallas as pl
from jax.experimental.pallas import tpu as pltpu
from jax.sharding import Mesh
from jax.sharding import PartitionSpec as P

HD = 128
TURN = 4
HEADS = 4
OWN = 16
REPL = ("z_lo", "y", "core")
TENS = ("z_hi", "x")
NREP = 32
NCOL = 4
SLOTS = 32
QROWS = HEADS * TURN
VM = pl.BlockSpec(memory_space=pltpu.VMEM)
SM = pl.BlockSpec(memory_space=pltpu.SMEM)
HBM = pl.BlockSpec(memory_space=pltpu.HBM)
ROOM = pltpu.CompilerParams(vmem_limit_bytes=16 << 20)


def route_kernel(own_ref, serve_hbm, q_hbm, k_hbm, v_hbm, out_ref, serve_ref, q_ref, k_ref, v_ref, sems):
    pairs = ((serve_hbm, serve_ref), (q_hbm, q_ref), (k_hbm, k_ref), (v_hbm, v_ref))
    copies = [pltpu.make_async_copy(src, dst, sems.at[n]) for n, (src, dst) in enumerate(pairs)]
    for copy in copies:
        copy.start()
    copies[0].wait()
    serve = serve_ref[...]
    chosen = jnp.where(serve // NREP == own_ref[0], serve % NREP, 0)
    index = [jnp.sum(chosen[r : r + 1, :]) for r in range(NREP)]
    for copy in copies[1:]:
        copy.wait()
    for r in range(NREP):
        i = index[r]
        rows = q_ref[i]
        for h in range(HEADS):
            out_ref[r, h * TURN : (h + 1) * TURN, :] = rows[:, h * HD : (h + 1) * HD]
        out_ref[r, QROWS : QROWS + TURN, :] = k_ref[i]
        out_ref[r, QROWS + TURN : QROWS + 2 * TURN, :] = v_ref[i]


def spread_kernel(w_ref, out_ref):
    blocks = w_ref.shape[2] // NCOL // HD
    for y in range(NCOL):
        for j in range(blocks):
            first = (y * blocks + j) * HD
            piece = w_ref[0, :, first : first + HD]
            for z in range(4):
                out_ref[z * NCOL + y, j * OWN : (j + 1) * OWN, :] = piece


def attend_kernel(own_ref, zhi_ref, serve_ref, turn_ref, cache_ref, got_ref, ck_ref, cv_ref, out_ref, nk, nv, s1, acc):
    own = own_ref[0]
    rows = SLOTS * QROWS
    scale = 1.0 / math.sqrt(HD)
    lane = lax.broadcasted_iota(jnp.int32, (QROWS, HD), 1)
    turn_pos = lax.broadcasted_iota(jnp.int32, (QROWS, HD), 0) % TURN
    queries = []
    for s in range(SLOTS):
        source = serve_ref[own, s] // NREP
        queries.append(got_ref[source, 0:QROWS, :])
        nk[s * TURN : (s + 1) * TURN, :] = got_ref[source, QROWS : QROWS + TURN, :]
        nv[s * TURN : (s + 1) * TURN, :] = got_ref[source, QROWS + TURN : QROWS + 2 * TURN, :]
        raw = lax.dot_general(queries[s], ck_ref[s], (((1,), (1,)), ((), ())), preferred_element_type=jnp.float32)
        s1[s * QROWS : (s + 1) * QROWS, :] = jnp.where(lane < cache_ref[s], raw * scale, -jnp.inf)
    all_q = jnp.concatenate(queries, axis=0)
    fresh = lax.dot_general(all_q, nk[...], (((1,), (1,)), ((), ())), preferred_element_type=jnp.float32)
    row = lax.broadcasted_iota(jnp.int32, (rows, SLOTS * TURN), 0)
    col = lax.broadcasted_iota(jnp.int32, (rows, SLOTS * TURN), 1)
    seen = (col // TURN == row // QROWS) & (col % TURN <= row % TURN)
    fresh = jnp.where(seen, fresh * scale, -jnp.inf)
    cached = s1[...]
    top = jnp.max(jnp.maximum(cached, fresh), axis=1, keepdims=True)
    e1 = jnp.exp(cached - top)
    e2 = jnp.exp(fresh - top)
    total = jnp.sum(e1 + e2, axis=1, keepdims=True)
    w1 = (e1 / total).astype(jnp.bfloat16)
    w2 = (e2 / total).astype(jnp.bfloat16)
    acc[...] = jnp.dot(w2, nv[...], preferred_element_type=jnp.float32)
    for s in range(SLOTS):
        part = slice(s * QROWS, (s + 1) * QROWS)
        mixed = acc[part, :] + jnp.dot(w1[part, :], cv_ref[s], preferred_element_type=jnp.float32)
        live = turn_ref[serve_ref[own, s]]
        mixed = jnp.where(turn_pos < live, mixed, 0.0).astype(jnp.bfloat16)
        t = s // 2
        x, at = t % 4, (s % 2) * TURN
        z = (t // 4 + 4 - zhi_ref[0]) % 4
        for h in range(HEADS):
            out_ref[x, z, at : at + TURN, h * HD : (h + 1) * HD] = mixed[h * TURN : (h + 1) * TURN, :]


def weight_kernel(owner_ref, core_ref, near_ref, far_ref, out_ref, both):
    core = core_ref[0]
    both[core] = near_ref[...]
    both[1 - core] = far_ref[...]
    for b in range(NREP):
        source = owner_ref[b]
        for j in range(out_ref.shape[1] // HD):
            piece = both[source % 2, source // 2, j * OWN : (j + 1) * OWN, :]
            out_ref[b * OWN : (b + 1) * OWN, j * HD : (j + 1) * HD] = piece


def matmul_kernel(rows_ref, w_ref, out_ref):
    product = jnp.dot(rows_ref[...], w_ref[...], preferred_element_type=jnp.float32).astype(jnp.bfloat16)
    for y in range(out_ref.shape[1]):
        for x in range(out_ref.shape[0]):
            first = (y * out_ref.shape[0] + x) * out_ref.shape[2]
            out_ref[x, y] = product[first : first + out_ref.shape[2], :]


def on_device(
    queries,
    new_keys,
    new_values,
    cache_keys,
    cache_values,
    serve_lists,
    turn_lens,
    cache_lens,
    owner_map,
    new_wo,
):
    own = lax.axis_index(REPL)
    out_width = new_wo.shape[2]
    width = out_width // NCOL
    core = lax.axis_index("core").reshape(1)
    routed = pl.pallas_call(
        route_kernel,
        out_shape=jax.ShapeDtypeStruct((NREP, QROWS + 2 * TURN, HD), jnp.bfloat16),
        in_specs=[SM, HBM, HBM, HBM, HBM],
        out_specs=VM,
        scratch_shapes=[
            pltpu.VMEM(serve_lists.shape, jnp.int32),
            pltpu.VMEM(queries.shape, jnp.bfloat16),
            pltpu.VMEM(new_keys.shape, jnp.bfloat16),
            pltpu.VMEM(new_values.shape, jnp.bfloat16),
            pltpu.SemaphoreType.DMA((4,)),
        ],
    )(own.reshape(1), serve_lists, queries, new_keys, new_values)
    pieces_shape = (NREP // 2, width // HD * OWN, HD)
    spread = pl.pallas_call(
        spread_kernel,
        out_shape=jax.ShapeDtypeStruct(pieces_shape, jnp.bfloat16),
        compiler_params=ROOM,
        in_specs=[VM],
        out_specs=VM,
        cost_estimate=pl.CostEstimate(flops=0, bytes_accessed=4 << 20, transcendentals=0),
    )(new_wo)
    got = lax.all_to_all(routed, REPL, split_axis=0, concat_axis=0, tiled=True)
    got, spread = lax.optimization_barrier((got, spread))
    pieces = lax.all_to_all(spread, ("z_lo", "y"), split_axis=0, concat_axis=0, tiled=True)
    attended = pl.pallas_call(
        attend_kernel,
        out_shape=jax.ShapeDtypeStruct((4, 4, 2 * TURN, HEADS * HD), jnp.bfloat16),
        compiler_params=ROOM,
        in_specs=[SM, SM, SM, SM, SM, VM, VM, VM],
        out_specs=VM,
        scratch_shapes=[
            pltpu.VMEM((SLOTS * TURN, HD), jnp.bfloat16),
            pltpu.VMEM((SLOTS * TURN, HD), jnp.bfloat16),
            pltpu.VMEM((SLOTS * QROWS, HD), jnp.float32),
            pltpu.VMEM((SLOTS * QROWS, HD), jnp.float32),
        ],
        cost_estimate=pl.CostEstimate(flops=1 << 30, bytes_accessed=8 << 20, transcendentals=1 << 17),
    )(own.reshape(1), lax.axis_index("z_hi").reshape(1), serve_lists, turn_lens, cache_lens, got, cache_keys, cache_values)
    rows = lax.all_gather(attended, "y", axis=0)
    rows, pieces = lax.optimization_barrier((rows, pieces))
    across = lax.ppermute(pieces, "core", [(0, 1), (1, 0)])
    weight = pl.pallas_call(
        weight_kernel,
        out_shape=jax.ShapeDtypeStruct((NREP * OWN, width), jnp.bfloat16),
        compiler_params=ROOM,
        in_specs=[SM, SM, VM, VM],
        out_specs=VM,
        scratch_shapes=[pltpu.VMEM((2,) + pieces_shape, jnp.bfloat16)],
        cost_estimate=pl.CostEstimate(flops=0, bytes_accessed=2 * 2 * NREP * OWN * width, transcendentals=0),
    )(owner_map, core, pieces, across)
    served = SLOTS * TURN
    partial = pl.pallas_call(
        matmul_kernel,
        out_shape=jax.ShapeDtypeStruct((4, NCOL, 8 * TURN, width), jnp.bfloat16),
        grid=(NCOL // 2,),
        compiler_params=ROOM,
        in_specs=[
            pl.BlockSpec((2 * served, HEADS * HD), lambda i: (i, 0)),
            pl.BlockSpec((NREP * OWN, width), lambda i: (0, 0)),
        ],
        out_specs=pl.BlockSpec((4, 2, 8 * TURN, width), lambda i: (0, i, 0, 0)),
    )(rows.reshape(NCOL * served, HEADS * HD), weight)
    partial = partial.reshape(NCOL * 4, 8 * TURN, width)
    over_x = lax.all_to_all(partial, ("x", "y"), split_axis=0, concat_axis=0, tiled=True)
    summed = jnp.sum(over_x.reshape(4, NCOL, 4, 2 * TURN, width).astype(jnp.float32), axis=0)
    summed = jnp.transpose(summed.astype(jnp.bfloat16), (1, 0, 2, 3))
    hops = [lax.ppermute(summed[d], "z_hi", [(i, (i + d) % 4) for i in range(4)]) for d in (2, 1, 3)]
    projected = sum(part.astype(jnp.float32) for part in [summed[0]] + hops).astype(jnp.bfloat16)
    return jnp.transpose(projected, (1, 0, 2)).reshape(1, 2 * TURN, out_width)


def solution(mesh):
    fine = Mesh(mesh.devices.reshape(4, 4, 2, 4, 4), REPL + TENS)
    placed = (
        P(REPL, None, TENS),
        P(REPL, None, TENS),
        P(REPL, None, TENS),
        P(REPL, None, TENS),
        P(REPL, None, TENS),
        P(),
        P(),
        P(REPL),
        P(),
        P(REPL, TENS, None),
    )
    return jax.shard_map(
        on_device,
        mesh=fine,
        in_specs=placed,
        out_specs=P(REPL, TENS, None),
        check_vma=False,
    )
```

```python
import math

import jax
import jax.numpy as jnp
from jax import lax
from jax.experimental import pallas as pl
from jax.experimental.pallas import tpu as pltpu
from jax.sharding import Mesh
from jax.sharding import PartitionSpec as P

HD = 128
TURN = 4
HEADS = 4
OWN = 16
REPL = ("z_lo", "y", "core")
TENS = ("z_hi", "x")
NREP = 32
NCOL = 4
SLOTS = 32
QROWS = HEADS * TURN
VM = pl.BlockSpec(memory_space=pltpu.VMEM)
SM = pl.BlockSpec(memory_space=pltpu.SMEM)
HBM = pl.BlockSpec(memory_space=pltpu.HBM)
ROOM = pltpu.CompilerParams(vmem_limit_bytes=16 << 20)


def route_kernel(own_ref, serve_hbm, q_hbm, k_hbm, v_hbm, out_ref, serve_ref, q_ref, k_ref, v_ref, sems):
    pairs = ((serve_hbm, serve_ref), (q_hbm, q_ref), (k_hbm, k_ref), (v_hbm, v_ref))
    copies = [pltpu.make_async_copy(src, dst, sems.at[n]) for n, (src, dst) in enumerate(pairs)]
    for copy in copies:
        copy.start()
    copies[0].wait()
    serve = serve_ref[...]
    chosen = jnp.where(serve // NREP == own_ref[0], serve % NREP, 0)
    index = [jnp.sum(chosen[r : r + 1, :]) for r in range(NREP)]
    for copy in copies[1:]:
        copy.wait()
    for r in range(NREP):
        i = index[r]
        rows = q_ref[i]
        for h in range(HEADS):
            out_ref[r, h * TURN : (h + 1) * TURN, :] = rows[:, h * HD : (h + 1) * HD]
        out_ref[r, QROWS : QROWS + TURN, :] = k_ref[i]
        out_ref[r, QROWS + TURN : QROWS + 2 * TURN, :] = v_ref[i]


def spread_kernel(w_ref, out_ref):
    blocks = w_ref.shape[2] // NCOL // HD
    for y in range(NCOL):
        for j in range(blocks):
            first = (y * blocks + j) * HD
            piece = w_ref[0, :, first : first + HD]
            for z in range(4):
                out_ref[z * NCOL + y, j * OWN : (j + 1) * OWN, :] = piece


def attend_kernel(own_ref, zhi_ref, serve_ref, turn_ref, cache_ref, got_ref, ck_ref, cv_ref, out_ref, nk, nv, s1, acc):
    own = own_ref[0]
    rows = SLOTS * QROWS
    scale = 1.0 / math.sqrt(HD)
    lane = lax.broadcasted_iota(jnp.int32, (QROWS, HD), 1)
    turn_pos = lax.broadcasted_iota(jnp.int32, (QROWS, HD), 0) % TURN
    queries = []
    for s in range(SLOTS):
        source = serve_ref[own, s] // NREP
        queries.append(got_ref[source, 0:QROWS, :])
        nk[s * TURN : (s + 1) * TURN, :] = got_ref[source, QROWS : QROWS + TURN, :]
        nv[s * TURN : (s + 1) * TURN, :] = got_ref[source, QROWS + TURN : QROWS + 2 * TURN, :]
        raw = lax.dot_general(queries[s], ck_ref[s], (((1,), (1,)), ((), ())), preferred_element_type=jnp.float32)
        s1[s * QROWS : (s + 1) * QROWS, :] = jnp.where(lane < cache_ref[s], raw * scale, -jnp.inf)
    all_q = jnp.concatenate(queries, axis=0)
    fresh = lax.dot_general(all_q, nk[...], (((1,), (1,)), ((), ())), preferred_element_type=jnp.float32)
    row = lax.broadcasted_iota(jnp.int32, (rows, SLOTS * TURN), 0)
    col = lax.broadcasted_iota(jnp.int32, (rows, SLOTS * TURN), 1)
    seen = (col // TURN == row // QROWS) & (col % TURN <= row % TURN)
    fresh = jnp.where(seen, fresh * scale, -jnp.inf)
    cached = s1[...]
    top = jnp.max(jnp.maximum(cached, fresh), axis=1, keepdims=True)
    e1 = jnp.exp(cached - top)
    e2 = jnp.exp(fresh - top)
    total = jnp.sum(e1 + e2, axis=1, keepdims=True)
    w1 = (e1 / total).astype(jnp.bfloat16)
    w2 = (e2 / total).astype(jnp.bfloat16)
    acc[...] = jnp.dot(w2, nv[...], preferred_element_type=jnp.float32)
    for s in range(SLOTS):
        part = slice(s * QROWS, (s + 1) * QROWS)
        mixed = acc[part, :] + jnp.dot(w1[part, :], cv_ref[s], preferred_element_type=jnp.float32)
        live = turn_ref[serve_ref[own, s]]
        mixed = jnp.where(turn_pos < live, mixed, 0.0).astype(jnp.bfloat16)
        t = s // 2
        x, at = t % 4, (s % 2) * TURN
        z = (t // 4 + 4 - zhi_ref[0]) % 4
        for h in range(HEADS):
            out_ref[x, z, at : at + TURN, h * HD : (h + 1) * HD] = mixed[h * TURN : (h + 1) * TURN, :]


def weight_kernel(owner_ref, core_ref, near_ref, far_ref, out_ref, both):
    core = core_ref[0]
    both[core] = near_ref[...]
    both[1 - core] = far_ref[...]
    for b in range(NREP):
        source = owner_ref[b]
        for j in range(out_ref.shape[1] // HD):
            piece = both[source % 2, source // 2, j * OWN : (j + 1) * OWN, :]
            out_ref[b * OWN : (b + 1) * OWN, j * HD : (j + 1) * HD] = piece


def matmul_kernel(rows_ref, w_ref, out_ref):
    product = jnp.dot(rows_ref[...], w_ref[...], preferred_element_type=jnp.float32).astype(jnp.bfloat16)
    for y in range(out_ref.shape[1]):
        for x in range(out_ref.shape[0]):
            first = (y * out_ref.shape[0] + x) * out_ref.shape[2]
            out_ref[x, y] = product[first : first + out_ref.shape[2], :]


def on_device(
    queries,
    new_keys,
    new_values,
    cache_keys,
    cache_values,
    serve_lists,
    turn_lens,
    cache_lens,
    owner_map,
    new_wo,
):
    own = lax.axis_index(REPL)
    out_width = new_wo.shape[2]
    width = out_width // NCOL
    core = lax.axis_index("core").reshape(1)
    routed = pl.pallas_call(
        route_kernel,
        out_shape=jax.ShapeDtypeStruct((NREP, QROWS + 2 * TURN, HD), jnp.bfloat16),
        in_specs=[SM, HBM, HBM, HBM, HBM],
        out_specs=VM,
        scratch_shapes=[
            pltpu.VMEM(serve_lists.shape, jnp.int32),
            pltpu.VMEM(queries.shape, jnp.bfloat16),
            pltpu.VMEM(new_keys.shape, jnp.bfloat16),
            pltpu.VMEM(new_values.shape, jnp.bfloat16),
            pltpu.SemaphoreType.DMA((4,)),
        ],
    )(own.reshape(1), serve_lists, queries, new_keys, new_values)
    pieces_shape = (NREP // 2, width // HD * OWN, HD)
    spread = pl.pallas_call(
        spread_kernel,
        out_shape=jax.ShapeDtypeStruct(pieces_shape, jnp.bfloat16),
        compiler_params=ROOM,
        in_specs=[VM],
        out_specs=VM,
        cost_estimate=pl.CostEstimate(flops=0, bytes_accessed=4 << 20, transcendentals=0),
    )(new_wo)
    got = lax.all_to_all(routed, REPL, split_axis=0, concat_axis=0, tiled=True)
    got, spread = lax.optimization_barrier((got, spread))
    pieces = lax.all_to_all(spread, ("z_lo", "y"), split_axis=0, concat_axis=0, tiled=True)
    attended = pl.pallas_call(
        attend_kernel,
        out_shape=jax.ShapeDtypeStruct((4, 4, 2 * TURN, HEADS * HD), jnp.bfloat16),
        compiler_params=ROOM,
        in_specs=[SM, SM, SM, SM, SM, VM, VM, VM],
        out_specs=VM,
        scratch_shapes=[
            pltpu.VMEM((SLOTS * TURN, HD), jnp.bfloat16),
            pltpu.VMEM((SLOTS * TURN, HD), jnp.bfloat16),
            pltpu.VMEM((SLOTS * QROWS, HD), jnp.float32),
            pltpu.VMEM((SLOTS * QROWS, HD), jnp.float32),
        ],
        cost_estimate=pl.CostEstimate(flops=1 << 30, bytes_accessed=8 << 20, transcendentals=1 << 17),
    )(own.reshape(1), lax.axis_index("z_hi").reshape(1), serve_lists, turn_lens, cache_lens, got, cache_keys, cache_values)
    rows = lax.all_gather(attended, "y", axis=0)
    rows, pieces = lax.optimization_barrier((rows, pieces))
    across = lax.ppermute(pieces, "core", [(0, 1), (1, 0)])
    weight = pl.pallas_call(
        weight_kernel,
        out_shape=jax.ShapeDtypeStruct((NREP * OWN, width), jnp.bfloat16),
        compiler_params=ROOM,
        in_specs=[SM, SM, VM, VM],
        out_specs=VM,
        scratch_shapes=[pltpu.VMEM((2,) + pieces_shape, jnp.bfloat16)],
        cost_estimate=pl.CostEstimate(flops=0, bytes_accessed=2 * 2 * NREP * OWN * width, transcendentals=0),
    )(owner_map, core, pieces, across)
    served = SLOTS * TURN
    partial = pl.pallas_call(
        matmul_kernel,
        out_shape=jax.ShapeDtypeStruct((4, NCOL, 8 * TURN, width), jnp.bfloat16),
        compiler_params=ROOM,
        in_specs=[VM, VM],
        out_specs=VM,
    )(rows.reshape(NCOL * served, HEADS * HD), weight)
    partial = partial.reshape(NCOL * 4, 8 * TURN, width)
    over_x = lax.all_to_all(partial, ("x", "y"), split_axis=0, concat_axis=0, tiled=True)
    summed = jnp.sum(over_x.reshape(4, NCOL, 4, 2 * TURN, width).astype(jnp.float32), axis=0)
    summed = jnp.transpose(summed.astype(jnp.bfloat16), (1, 0, 2, 3))
    hops = [lax.ppermute(summed[d], "z_hi", [(i, (i + d) % 4) for i in range(4)]) for d in (2, 1, 3)]
    projected = sum(part.astype(jnp.float32) for part in [summed[0]] + hops).astype(jnp.bfloat16)
    return jnp.transpose(projected, (1, 0, 2)).reshape(1, 2 * TURN, out_width)


def solution(mesh):
    fine = Mesh(mesh.devices.reshape(4, 4, 2, 4, 4), REPL + TENS)
    placed = (
        P(REPL, None, TENS),
        P(REPL, None, TENS),
        P(REPL, None, TENS),
        P(REPL, None, TENS),
        P(REPL, None, TENS),
        P(),
        P(),
        P(REPL),
        P(),
        P(REPL, TENS, None),
    )
    return jax.shard_map(
        on_device,
        mesh=fine,
        in_specs=placed,
        out_specs=P(REPL, TENS, None),
        check_vma=False,
    )
```

```python
import math

import jax
import jax.numpy as jnp
from jax import lax
from jax.experimental import pallas as pl
from jax.experimental.pallas import tpu as pltpu
from jax.sharding import Mesh
from jax.sharding import PartitionSpec as P

HD = 128
TURN = 4
HEADS = 4
OWN = 16
REPL = ("z_lo", "y", "core")
TENS = ("z_hi", "x")
NREP = 32
NCOL = 4
SLOTS = 32
QROWS = HEADS * TURN
VM = pl.BlockSpec(memory_space=pltpu.VMEM)
SM = pl.BlockSpec(memory_space=pltpu.SMEM)
HBM = pl.BlockSpec(memory_space=pltpu.HBM)
ROOM = pltpu.CompilerParams(vmem_limit_bytes=16 << 20)


def route_kernel(own_ref, serve_hbm, q_hbm, k_hbm, v_hbm, out_ref, serve_ref, q_ref, k_ref, v_ref, sems):
    pairs = ((serve_hbm, serve_ref), (q_hbm, q_ref), (k_hbm, k_ref), (v_hbm, v_ref))
    copies = [pltpu.make_async_copy(src, dst, sems.at[n]) for n, (src, dst) in enumerate(pairs)]
    for copy in copies:
        copy.start()
    copies[0].wait()
    serve = serve_ref[...]
    chosen = jnp.where(serve // NREP == own_ref[0], serve % NREP, 0)
    index = [jnp.sum(chosen[r : r + 1, :]) for r in range(NREP)]
    for copy in copies[1:]:
        copy.wait()
    for r in range(NREP):
        i = index[r]
        rows = q_ref[i]
        for h in range(HEADS):
            out_ref[r, h * TURN : (h + 1) * TURN, :] = rows[:, h * HD : (h + 1) * HD]
        out_ref[r, QROWS : QROWS + TURN, :] = k_ref[i]
        out_ref[r, QROWS + TURN : QROWS + 2 * TURN, :] = v_ref[i]


def spread_kernel(w_ref, out_ref):
    blocks = w_ref.shape[2] // NCOL // HD
    for y in range(NCOL):
        for j in range(blocks):
            first = (y * blocks + j) * HD
            piece = w_ref[0, :, first : first + HD]
            for z in range(4):
                out_ref[y * 4 + z, j * OWN : (j + 1) * OWN, :] = piece


def attend_kernel(own_ref, zhi_ref, serve_ref, turn_ref, cache_ref, got_ref, ck_ref, cv_ref, out_ref, nk, nv, s1, acc):
    own = own_ref[0]
    rows = SLOTS * QROWS
    scale = 1.0 / math.sqrt(HD)
    lane = lax.broadcasted_iota(jnp.int32, (QROWS, HD), 1)
    turn_pos = lax.broadcasted_iota(jnp.int32, (QROWS, HD), 0) % TURN
    queries = []
    for s in range(SLOTS):
        source = serve_ref[own, s] // NREP
        queries.append(got_ref[source, 0:QROWS, :])
        nk[s * TURN : (s + 1) * TURN, :] = got_ref[source, QROWS : QROWS + TURN, :]
        nv[s * TURN : (s + 1) * TURN, :] = got_ref[source, QROWS + TURN : QROWS + 2 * TURN, :]
        raw = lax.dot_general(queries[s], ck_ref[s], (((1,), (1,)), ((), ())), preferred_element_type=jnp.float32)
        s1[s * QROWS : (s + 1) * QROWS, :] = jnp.where(lane < cache_ref[s], raw * scale, -jnp.inf)
    all_q = jnp.concatenate(queries, axis=0)
    fresh = lax.dot_general(all_q, nk[...], (((1,), (1,)), ((), ())), preferred_element_type=jnp.float32)
    row = lax.broadcasted_iota(jnp.int32, (rows, SLOTS * TURN), 0)
    col = lax.broadcasted_iota(jnp.int32, (rows, SLOTS * TURN), 1)
    seen = (col // TURN == row // QROWS) & (col % TURN <= row % TURN)
    fresh = jnp.where(seen, fresh * scale, -jnp.inf)
    cached = s1[...]
    top = jnp.max(jnp.maximum(cached, fresh), axis=1, keepdims=True)
    e1 = jnp.exp(cached - top)
    e2 = jnp.exp(fresh - top)
    total = jnp.sum(e1 + e2, axis=1, keepdims=True)
    w1 = (e1 / total).astype(jnp.bfloat16)
    w2 = (e2 / total).astype(jnp.bfloat16)
    acc[...] = jnp.dot(w2, nv[...], preferred_element_type=jnp.float32)
    for s in range(SLOTS):
        part = slice(s * QROWS, (s + 1) * QROWS)
        mixed = acc[part, :] + jnp.dot(w1[part, :], cv_ref[s], preferred_element_type=jnp.float32)
        live = turn_ref[serve_ref[own, s]]
        mixed = jnp.where(turn_pos < live, mixed, 0.0).astype(jnp.bfloat16)
        t = s // 2
        x, at = t % 4, (s % 2) * TURN
        z = (t // 4 + 4 - zhi_ref[0]) % 4
        for h in range(HEADS):
            out_ref[x, z, at : at + TURN, h * HD : (h + 1) * HD] = mixed[h * TURN : (h + 1) * TURN, :]


def weight_kernel(owner_ref, core_ref, near_ref, far_ref, out_ref, both):
    core = core_ref[0]
    both[core] = near_ref[...]
    both[1 - core] = far_ref[...]
    for b in range(NREP):
        source = owner_ref[b]
        for j in range(out_ref.shape[1] // HD):
            piece = both[source % 2, source // 2 % NCOL * 4 + source // (2 * NCOL), j * OWN : (j + 1) * OWN, :]
            out_ref[b * OWN : (b + 1) * OWN, j * HD : (j + 1) * HD] = piece


def matmul_kernel(rows_ref, w_ref, out_ref):
    product = jnp.dot(rows_ref[...], w_ref[...], preferred_element_type=jnp.float32).astype(jnp.bfloat16)
    for y in range(out_ref.shape[1]):
        for x in range(out_ref.shape[0]):
            first = (y * out_ref.shape[0] + x) * out_ref.shape[2]
            out_ref[x, y] = product[first : first + out_ref.shape[2], :]


def on_device(
    queries,
    new_keys,
    new_values,
    cache_keys,
    cache_values,
    serve_lists,
    turn_lens,
    cache_lens,
    owner_map,
    new_wo,
):
    own = lax.axis_index(REPL)
    out_width = new_wo.shape[2]
    width = out_width // NCOL
    core = lax.axis_index("core").reshape(1)
    routed = pl.pallas_call(
        route_kernel,
        out_shape=jax.ShapeDtypeStruct((NREP, QROWS + 2 * TURN, HD), jnp.bfloat16),
        in_specs=[SM, HBM, HBM, HBM, HBM],
        out_specs=VM,
        scratch_shapes=[
            pltpu.VMEM(serve_lists.shape, jnp.int32),
            pltpu.VMEM(queries.shape, jnp.bfloat16),
            pltpu.VMEM(new_keys.shape, jnp.bfloat16),
            pltpu.VMEM(new_values.shape, jnp.bfloat16),
            pltpu.SemaphoreType.DMA((4,)),
        ],
    )(own.reshape(1), serve_lists, queries, new_keys, new_values)
    pieces_shape = (NREP // 2, width // HD * OWN, HD)
    spread = pl.pallas_call(
        spread_kernel,
        out_shape=jax.ShapeDtypeStruct(pieces_shape, jnp.bfloat16),
        compiler_params=ROOM,
        in_specs=[VM],
        out_specs=VM,
        cost_estimate=pl.CostEstimate(flops=0, bytes_accessed=4 << 20, transcendentals=0),
    )(new_wo)
    got = lax.all_to_all(routed, REPL, split_axis=0, concat_axis=0, tiled=True)
    got, spread = lax.optimization_barrier((got, spread))
    pieces = lax.all_to_all(spread, ("y", "z_lo"), split_axis=0, concat_axis=0, tiled=True)
    attended = pl.pallas_call(
        attend_kernel,
        out_shape=jax.ShapeDtypeStruct((4, 4, 2 * TURN, HEADS * HD), jnp.bfloat16),
        compiler_params=ROOM,
        in_specs=[SM, SM, SM, SM, SM, VM, VM, VM],
        out_specs=VM,
        scratch_shapes=[
            pltpu.VMEM((SLOTS * TURN, HD), jnp.bfloat16),
            pltpu.VMEM((SLOTS * TURN, HD), jnp.bfloat16),
            pltpu.VMEM((SLOTS * QROWS, HD), jnp.float32),
            pltpu.VMEM((SLOTS * QROWS, HD), jnp.float32),
        ],
        cost_estimate=pl.CostEstimate(flops=1 << 30, bytes_accessed=8 << 20, transcendentals=1 << 17),
    )(own.reshape(1), lax.axis_index("z_hi").reshape(1), serve_lists, turn_lens, cache_lens, got, cache_keys, cache_values)
    rows = lax.all_gather(attended, "y", axis=0)
    rows, pieces = lax.optimization_barrier((rows, pieces))
    across = lax.ppermute(pieces, "core", [(0, 1), (1, 0)])
    weight = pl.pallas_call(
        weight_kernel,
        out_shape=jax.ShapeDtypeStruct((NREP * OWN, width), jnp.bfloat16),
        compiler_params=ROOM,
        in_specs=[SM, SM, VM, VM],
        out_specs=VM,
        scratch_shapes=[pltpu.VMEM((2,) + pieces_shape, jnp.bfloat16)],
        cost_estimate=pl.CostEstimate(flops=0, bytes_accessed=2 * 2 * NREP * OWN * width, transcendentals=0),
    )(owner_map, core, pieces, across)
    served = SLOTS * TURN
    partial = pl.pallas_call(
        matmul_kernel,
        out_shape=jax.ShapeDtypeStruct((4, NCOL, 8 * TURN, width), jnp.bfloat16),
        grid=(NCOL // 2,),
        compiler_params=ROOM,
        in_specs=[
            pl.BlockSpec((2 * served, HEADS * HD), lambda i: (i, 0)),
            pl.BlockSpec((NREP * OWN, width), lambda i: (0, 0)),
        ],
        out_specs=pl.BlockSpec((4, 2, 8 * TURN, width), lambda i: (0, i, 0, 0)),
    )(rows.reshape(NCOL * served, HEADS * HD), weight)
    partial = partial.reshape(NCOL * 4, 8 * TURN, width)
    over_x = lax.all_to_all(partial, ("x", "y"), split_axis=0, concat_axis=0, tiled=True)
    summed = jnp.sum(over_x.reshape(4, NCOL, 4, 2 * TURN, width).astype(jnp.float32), axis=0)
    summed = jnp.transpose(summed.astype(jnp.bfloat16), (1, 0, 2, 3))
    hops = [lax.ppermute(summed[d], "z_hi", [(i, (i + d) % 4) for i in range(4)]) for d in (2, 1, 3)]
    projected = sum(part.astype(jnp.float32) for part in [summed[0]] + hops).astype(jnp.bfloat16)
    return jnp.transpose(projected, (1, 0, 2)).reshape(1, 2 * TURN, out_width)


def solution(mesh):
    fine = Mesh(mesh.devices.reshape(4, 4, 2, 4, 4), REPL + TENS)
    placed = (
        P(REPL, None, TENS),
        P(REPL, None, TENS),
        P(REPL, None, TENS),
        P(REPL, None, TENS),
        P(REPL, None, TENS),
        P(),
        P(),
        P(REPL),
        P(),
        P(REPL, TENS, None),
    )
    return jax.shard_map(
        on_device,
        mesh=fine,
        in_specs=placed,
        out_specs=P(REPL, TENS, None),
        check_vma=False,
    )
```
